32 devices in a mesh: groups: 2 (over y), row: 16 (over z, x, core).
Axes of the slice: x: 2, y: 2, z: 4, core: 2. Of those that a mesh axis runs over, the one named last changes fastest.
Arguments:
- grad: bfloat16 [512, 15360], P(('groups', 'row')), parts along dimension 0, may hold values from -0.875 to 0.875
- stats: float32 [256, 1024, 1024], P(('groups', 'row')), parts along dimension 0, may hold values from -6 to 6
- roots: bfloat16 [256, 1024, 1024], P(('groups', 'row')), parts along dimension 0, may hold values from -0.1875 to 0.1875
- tile_slot: int32 [128], replicated, may hold values from -1 to 119, as said below
Outputs:
- new_stats: float32 [256, 1024, 1024], P(('groups', 'row')), parts along dimension 0
- precond: bfloat16 [512, 15360], P(('groups', 'row')), parts along dimension 0
The draws below stay inside these ranges and needn't reach their ends.
There are 2 independent parts, one for each index of `groups`. The reference program is written for one: setup_inputs(seed, part) draws one part's arguments, and reference() takes and returns one part's arrays. A program takes and returns all parts, laid end to end along the dimension named above; an argument that names none is the same for every part. Nothing has to cross between parts.
Inputs may be any that keep to these rules, and one draw needn't show every extreme that they name: `tile_slot`: every number 0 to 119 appears exactly once; -1 marks an empty slot.
All inputs are finite; a program needn't handle non-finite values.
Results may differ from the reference program's by a relative error of at most 0.0049.
Values may be sent and summed in bfloat16 or wider, within the bound.
No kernel may reach another device: no remote copies, remote signals or barrier semaphores. Data moves between devices by JAX's collectives and lax.ppermute only.
A program may use at most 256 MiB of HBM per device.

```python
import jax
import jax.numpy as jnp
import numpy as np
from jax import lax

TILE = 1024
GRID = 15
ORDER = 15360
COLS = 256
NTILES = 120
SLOTALL = 128


def draw_tile_slot(key, part):
    filled = jnp.concatenate((jnp.arange(NTILES, dtype=jnp.int32), jnp.full((SLOTALL - NTILES,), -1, jnp.int32)))
    shuffle = jax.random.permutation(key, SLOTALL)
    return filled[shuffle]


def shard_levels(own_key, shape, shards, low, largest):
    def one(position, shards_of):
        steps = jax.random.uniform(jax.random.fold_in(jax.random.fold_in(own_key, 6), position), (shards_of,), jnp.float32, low / len(shards), largest / len(shards))
        return jnp.repeat(jnp.exp(steps), shape[position] // shards_of).reshape((-1,) + (1,) * (len(shape) - position - 1))

    gain = one(*shards[0])
    for cut in shards[1:]:
        gain = gain * one(*cut)
    return gain


def normal_values(stream_key, shape, scale, reach, shards=(), kind=jnp.bfloat16):
    values = scale * jax.random.normal(stream_key, shape, jnp.float32)
    if shards:
        values = values * shard_levels(stream_key, shape, shards, -0.22, 0.18)
    return jnp.clip(values, -reach, reach).astype(kind)


def setup_inputs(seed: int = 0, part: int = 0) -> dict:
    seeds = jax.random.split(jax.random.key(seed), 5)
    part_splits = jax.random.split(jax.random.fold_in(seeds[4], part), 5)
    grad = normal_values(part_splits[0], (COLS, ORDER), 0.15, 0.875, ((0, 16),))
    stats = normal_values(part_splits[1], (SLOTALL, TILE, TILE), 1.0, 6.0, ((0, 16),), jnp.float32)
    roots = normal_values(part_splits[2], (SLOTALL, TILE, TILE), TILE ** -0.5, 0.1875, ((0, 16),))
    tile_slot = draw_tile_slot(jax.random.fold_in(seeds[4], 71), part)
    return {"grad": grad, "stats": stats, "roots": roots, "tile_slot": tile_slot}


BETA = 0.9


def tile_tables(grid_len):
    first_list = []
    second_list = []
    for row_index in range(grid_len):
        for col_index in range(row_index, grid_len):
            first_list.append(row_index)
            second_list.append(col_index)
    return np.array(first_list, np.int32), np.array(second_list, np.int32)


def lookup(tile_slot, grid_len):
    first_table, second_table = tile_tables(grid_len)
    tile_total = first_table.shape[0]
    clipped = jnp.maximum(tile_slot, 0)
    matches = clipped[:, None] == jnp.arange(tile_total, dtype=jnp.int32)[None, :]
    first_panel = jnp.sum(jnp.where(matches, jnp.asarray(first_table)[None, :], 0), axis=1).astype(jnp.int32)
    second_panel = jnp.sum(jnp.where(matches, jnp.asarray(second_table)[None, :], 0), axis=1).astype(jnp.int32)
    return first_panel, second_panel, tile_slot >= 0


def reference(grad, stats, roots, tile_slot):
    first_panel, second_panel, live_mask = lookup(tile_slot, GRID)
    panels = grad.astype(jnp.float32).reshape(COLS, GRID, TILE)
    highest = lax.Precision.HIGHEST

    def advance(panels_sum, pieces):
        old_stat, root_tile, index_first, index_second, is_live = pieces
        grad_first = lax.dynamic_index_in_dim(panels, index_first, 1, keepdims=False)
        grad_second = lax.dynamic_index_in_dim(panels, index_second, 1, keepdims=False)
        products = jnp.dot(grad_first.T, grad_second, precision=highest, preferred_element_type=jnp.float32)
        updated = jnp.where(is_live, BETA * old_stat + (1.0 - BETA) * products, old_stat)
        keep_first = is_live.astype(jnp.float32)
        keep_second = (is_live & (index_first != index_second)).astype(jnp.float32)
        root_full = root_tile.astype(jnp.float32)
        part_first = (jnp.dot(grad_second, root_full.T, precision=highest, preferred_element_type=jnp.float32) * keep_first).astype(jnp.bfloat16)
        part_second = (jnp.dot(grad_first, root_full, precision=highest, preferred_element_type=jnp.float32) * keep_second).astype(jnp.bfloat16)
        current = lax.dynamic_index_in_dim(panels_sum, index_first, 1, keepdims=False)
        panels_sum = lax.dynamic_update_index_in_dim(panels_sum, current + part_first.astype(jnp.float32), index_first, 1)
        current = lax.dynamic_index_in_dim(panels_sum, index_second, 1, keepdims=False)
        panels_sum = lax.dynamic_update_index_in_dim(panels_sum, current + part_second.astype(jnp.float32), index_second, 1)
        return panels_sum, updated

    start_sum = jnp.zeros((COLS, GRID, TILE), jnp.float32)
    panels_sum, new_stats = lax.scan(advance, start_sum, (stats, roots, first_panel, second_panel, live_mask))
    return new_stats, panels_sum.reshape(COLS, ORDER).astype(jnp.bfloat16)
```

```python
import functools

import jax
import jax.numpy as jnp
from jax import lax
from jax.experimental import pallas as pl
from jax.experimental.pallas import tpu as pltpu
from jax.sharding import PartitionSpec as P

BETA = 0.9
F32 = jnp.float32
BF16 = jnp.bfloat16


def panels_of(tiles, grid_len):
    number = jnp.maximum(tiles, 0)
    first = jnp.zeros_like(number)
    for row_index in range(1, grid_len):
        first = first + (number >= row_index * grid_len - row_index * (row_index - 1) // 2)
    start = first * grid_len - first * (first - 1) // 2
    return first, number - start + first, (tiles >= 0).astype(jnp.int32)


def chip_cycle(chips):
    slow = 4 if chips % 4 == 0 else 1
    fast = chips // slow
    walk = [(row, 0) for row in range(slow)]
    for step, row in enumerate(reversed(range(slow))):
        span = range(1, fast) if step % 2 == 0 else reversed(range(1, fast))
        walk += [(row, col) for col in span]
    return [row * fast + col for row, col in walk]


def slab(refs, start, size):
    columns = pl.ds(pl.multiple_of(start, size), size)
    return jnp.concatenate([ref[:, columns] for ref in refs], 0)


def part_kernel(count, first_ref, second_ref, live_ref, own_ref, *refs):
    rest, root_ref, outs = refs[: count - 1], refs[count - 1], refs[count : 2 * count]
    acc, held, own, sems, own_sem = refs[2 * count :]
    slots, tile, _ = root_ref.shape
    depth = held.shape[0]
    grads = [*rest, own]

    def fetch(slot):
        at = lax.rem(slot, depth)
        return pltpu.make_async_copy(root_ref.at[slot], held.at[at], sems.at[at])

    own_copy = pltpu.make_async_copy(own_ref, own, own_sem)
    own_copy.start()
    for slot in range(min(depth, slots)):
        fetch(slot).start()
    acc[...] = jnp.zeros_like(acc)
    own_copy.wait()

    def step(slot, _):
        fetch(slot).wait()
        at = lax.rem(slot, depth)
        first, second = first_ref[slot] * tile, second_ref[slot] * tile

        @pl.when(live_ref[slot] > 0)
        def _():
            part = lax.dot_general(
                slab(grads, second, tile), held[at], (((1,), (1,)), ((), ())), preferred_element_type=F32
            )
            acc[:, pl.ds(pl.multiple_of(first, tile), tile)] += part.astype(BF16).astype(F32)

        @pl.when((live_ref[slot] > 0) & (first != second))
        def _():
            part = lax.dot_general(
                slab(grads, first, tile), held[at], (((1,), (0,)), ((), ())), preferred_element_type=F32
            )
            acc[:, pl.ds(pl.multiple_of(second, tile), tile)] += part.astype(BF16).astype(F32)

        @pl.when(slot + depth < slots)
        def _():
            fetch(slot + depth).start()

        return 0

    lax.fori_loop(0, slots, step, 0)
    at = 0
    for out in outs:
        out[...] = acc[at : at + out.shape[0], :].astype(BF16)
        at += out.shape[0]


SMEM_SPEC = pl.BlockSpec(memory_space=pltpu.SMEM)
VMEM_SPEC = pl.BlockSpec(memory_space=pltpu.VMEM)
ANY_SPEC = pl.BlockSpec(memory_space=pl.ANY)
HBM_SPEC = pl.BlockSpec(memory_space=pltpu.HBM)


def partial_sums(tables, own, rest, roots):
    slots, tile, _ = roots.shape
    order = own.shape[1]
    kinds = [*rest, own]
    rows = sum(g.shape[0] for g in kinds)
    depth = 2
    return pl.pallas_call(
        functools.partial(part_kernel, len(kinds)),
        out_shape=[jax.ShapeDtypeStruct(g.shape, BF16) for g in kinds],
        in_specs=[SMEM_SPEC] * 3 + [HBM_SPEC] + [VMEM_SPEC] * len(rest) + [ANY_SPEC],
        out_specs=[VMEM_SPEC] * len(kinds),
        scratch_shapes=[
            pltpu.VMEM((rows, order), F32),
            pltpu.VMEM((depth, tile, tile), BF16),
            pltpu.VMEM(own.shape, BF16),
            pltpu.SemaphoreType.DMA((depth,)),
            pltpu.SemaphoreType.DMA,
        ],
        compiler_params=pltpu.CompilerParams(vmem_limit_bytes=34 << 20),
        cost_estimate=pl.CostEstimate(
            flops=slots * 4 * rows * tile * tile, bytes_accessed=2 * slots * tile * tile, transcendentals=0
        ),
    )(*tables, own, *rest, roots)


def stat_kernel(count, base, length, first_ref, second_ref, live_ref, own_ref, *refs):
    rest, stat_ref = refs[: count - 1], refs[count - 1]
    out_ref, taken, made, own, in_sems, out_sems, own_sem = refs[-7:]
    depth, height, tile = taken.shape
    cut = tile // height
    total = length * cut
    grads = [*rest, own]

    def piece(ref, i):
        return ref.at[base + i // cut, pl.ds(pl.multiple_of(lax.rem(i, cut) * height, height), height), :]

    def fetch(i):
        at = lax.rem(i, depth)
        return pltpu.make_async_copy(piece(stat_ref, i), taken.at[at], in_sems.at[at])

    def store(i):
        at = lax.rem(i, depth)
        return pltpu.make_async_copy(made.at[at], piece(out_ref, i), out_sems.at[at])

    own_copy = pltpu.make_async_copy(own_ref, own, own_sem)
    own_copy.start()
    for i in range(min(depth, total)):
        fetch(i).start()
    own_copy.wait()

    def step(i, _):
        at = lax.rem(i, depth)
        slot = base + i // cut
        fetch(i).wait()

        @pl.when(i >= depth)
        def _():
            store(i - depth).wait()

        @pl.when(live_ref[slot] > 0)
        def _():
            left = slab(grads, first_ref[slot] * tile + lax.rem(i, cut) * height, height)
            right = slab(grads, second_ref[slot] * tile, tile)
            product = lax.dot_general(left, right, (((0,), (0,)), ((), ())), preferred_element_type=F32)
            made[at] = BETA * taken[at] + (1.0 - BETA) * product

        @pl.when(live_ref[slot] <= 0)
        def _():
            made[at] = taken[at]

        store(i).start()

        @pl.when(i + depth < total)
        def _():
            fetch(i + depth).start()

        return 0

    lax.fori_loop(0, total, step, 0)
    for i in range(max(total - depth, 0), total):
        store(i).wait()


def update_stats(tables, own, rest, stats, base, length, done):
    slots, tile, _ = stats.shape
    rows = own.shape[0] + sum(g.shape[0] for g in rest)
    depth, height = 4, tile // 4
    operands = [*tables, own, *rest, stats]
    in_specs = [SMEM_SPEC] * 3 + [HBM_SPEC] + [VMEM_SPEC] * len(rest) + [ANY_SPEC]
    aliases = {}
    if done is not None:
        aliases = {len(operands): 0}
        operands.append(done)
        in_specs.append(ANY_SPEC)
    return pl.pallas_call(
        functools.partial(stat_kernel, 1 + len(rest), base, length),
        out_shape=jax.ShapeDtypeStruct(stats.shape, F32),
        in_specs=in_specs,
        out_specs=ANY_SPEC,
        scratch_shapes=[
            pltpu.VMEM((depth, height, tile), F32),
            pltpu.VMEM((depth, height, tile), F32),
            pltpu.VMEM(own.shape, BF16),
            pltpu.SemaphoreType.DMA((depth,)),
            pltpu.SemaphoreType.DMA((depth,)),
            pltpu.SemaphoreType.DMA,
        ],
        input_output_aliases=aliases,
        compiler_params=pltpu.CompilerParams(vmem_limit_bytes=34 << 20),
        cost_estimate=pl.CostEstimate(
            flops=length * 2 * rows * tile * tile, bytes_accessed=8 * length * tile * tile, transcendentals=0
        ),
    )(*operands)


def body(grad, stats, roots, tile_slot):
    width, order = grad.shape
    slots, tile, _ = stats.shape
    devices = lax.axis_size("row")
    chips, half = devices // 2, width // 2
    mine = lax.dynamic_slice_in_dim(tile_slot, lax.axis_index("row") * slots, slots)
    tables = panels_of(mine, order // tile)

    if half % 8:
        everything = lax.all_gather(grad, "row", axis=0, tiled=True)
        (sums,) = partial_sums(tables, everything, [], roots)
        new_stats = update_stats(tables, everything, [], stats, 0, slots, None)
        total = lax.psum_scatter(sums.astype(F32), "row", scatter_dimension=0, tiled=True)
        return new_stats, total.astype(BF16)

    walk = chip_cycle(chips)
    forward, backward = [], []
    for here, there in zip(walk, walk[1:] + walk[:1]):
        for core in range(2):
            forward.append((2 * here + core, 2 * there + core))
            backward.append((2 * there + core, 2 * here + core))
    ahead = lambda v: lax.ppermute(v, "row", forward)
    back = lambda v: lax.ppermute(v, "row", backward)
    swap = lambda v: lax.ppermute(v, "row", [(i, i ^ 1) for i in range(devices)])

    reach = (chips - 1) // 2
    chunk = {0: grad}
    for step in range(1, reach + 1):
        chunk[-step], chunk[step] = ahead(chunk[1 - step]), back(chunk[step - 1])
        if step == 1:
            chunk[-1], tables = lax.optimization_barrier((chunk[-1], tables))
    chunk["low"], chunk["high"] = ahead(chunk[-reach][:half]), back(chunk[reach][half:])
    names = ["low", "high"]
    for step in range(reach, 0, -1):
        names += [-step, step]
    rest = [swap(chunk[k]) for k in [*names, 0]] + [chunk[k] for k in names]
    outs = partial_sums(tables, grad, rest, roots)
    names.append(0)
    other, own = dict(zip(names, outs)), dict(zip(names, outs[len(names) :]))

    here = lambda k: own[k].astype(F32) + swap(other[k]).astype(F32)
    sent = here("low").astype(BF16), here("high").astype(BF16)
    shares = [slots * part // 8 for part in (0, 1, 3, 6, 8)] if reach == 3 else [0] * (reach + 1) + [slots]
    done = None
    for step in range(reach, -1, -1):
        low, high = back(sent[0]), ahead(sent[1])
        base, stop = shares[reach - step : reach - step + 2]
        if stop > base:
            now = lax.optimization_barrier((*tables, *sent))[: len(tables)]
            done = update_stats(now, grad, rest, stats, base, stop - base, done)
            low, high, done = lax.optimization_barrier((low, high, done))
        low, high = low.astype(F32), high.astype(F32)
        if step == reach:
            low = jnp.pad(low, ((0, width - half), (0, 0)))
            high = jnp.pad(high, ((half, 0), (0, 0)))
        if step:
            sent = (here(-step) + low).astype(BF16), (here(step) + high).astype(BF16)
    return done, (here(0) + low + high).astype(BF16)


def solution(mesh):
    placed = (
        P(("groups", "row"), None),
        P(("groups", "row"), None, None),
        P(("groups", "row"), None, None),
        P(),
    )
    return jax.shard_map(
        body,
        mesh=mesh,
        in_specs=placed,
        out_specs=(P(("groups", "row"), None, None), P(("groups", "row"), None)),
        check_vma=False,
    )
```

```python
import functools

import jax
import jax.numpy as jnp
from jax import lax
from jax.experimental import pallas as pl
from jax.experimental.pallas import tpu as pltpu
from jax.sharding import PartitionSpec as P

BETA = 0.9
F32 = jnp.float32
BF16 = jnp.bfloat16


def panels_of(tiles, grid_len):
    number = jnp.maximum(tiles, 0)
    first = jnp.zeros_like(number)
    for row_index in range(1, grid_len):
        first = first + (number >= row_index * grid_len - row_index * (row_index - 1) // 2)
    start = first * grid_len - first * (first - 1) // 2
    return first, number - start + first, (tiles >= 0).astype(jnp.int32)


def chip_cycle(chips):
    slow = 4 if chips % 4 == 0 else 1
    fast = chips // slow
    walk = [(row, 0) for row in range(slow)]
    for step, row in enumerate(reversed(range(slow))):
        span = range(1, fast) if step % 2 == 0 else reversed(range(1, fast))
        walk += [(row, col) for col in span]
    return [row * fast + col for row, col in walk]


def slab(refs, start, size):
    columns = pl.ds(pl.multiple_of(start, size), size)
    return jnp.concatenate([ref[:, columns] for ref in refs], 0)


def part_kernel(count, first_ref, second_ref, live_ref, *refs):
    grads, root_ref, outs = refs[:count], refs[count], refs[count + 1 : -3]
    acc, held, sems = refs[-3:]
    slots, tile, _ = root_ref.shape
    depth = held.shape[0]

    def fetch(slot):
        at = lax.rem(slot, depth)
        return pltpu.make_async_copy(root_ref.at[slot], held.at[at], sems.at[at])

    for slot in range(min(depth, slots)):
        fetch(slot).start()
    acc[...] = jnp.zeros_like(acc)

    def step(slot, _):
        fetch(slot).wait()
        at = lax.rem(slot, depth)
        first, second = first_ref[slot] * tile, second_ref[slot] * tile

        @pl.when(live_ref[slot] > 0)
        def _():
            part = lax.dot_general(
                slab(grads, second, tile), held[at], (((1,), (1,)), ((), ())), preferred_element_type=F32
            )
            acc[:, pl.ds(pl.multiple_of(first, tile), tile)] += part.astype(BF16).astype(F32)

        @pl.when((live_ref[slot] > 0) & (first != second))
        def _():
            part = lax.dot_general(
                slab(grads, first, tile), held[at], (((1,), (0,)), ((), ())), preferred_element_type=F32
            )
            acc[:, pl.ds(pl.multiple_of(second, tile), tile)] += part.astype(BF16).astype(F32)

        @pl.when(slot + depth < slots)
        def _():
            fetch(slot + depth).start()

        return 0

    lax.fori_loop(0, slots, step, 0)
    at = 0
    for out in outs:
        out[...] = acc[at : at + out.shape[0], :].astype(BF16)
        at += out.shape[0]


SMEM_SPEC = pl.BlockSpec(memory_space=pltpu.SMEM)
VMEM_SPEC = pl.BlockSpec(memory_space=pltpu.VMEM)
ANY_SPEC = pl.BlockSpec(memory_space=pl.ANY)
HBM_SPEC = pl.BlockSpec(memory_space=pltpu.HBM)


def partial_sums(tables, grads, heights, roots):
    slots, tile, _ = roots.shape
    rows, order = sum(heights), grads[0].shape[1]
    depth = 2
    return pl.pallas_call(
        functools.partial(part_kernel, len(grads)),
        out_shape=[jax.ShapeDtypeStruct((height, order), BF16) for height in heights],
        in_specs=[SMEM_SPEC] * 3 + [VMEM_SPEC] * len(grads) + [ANY_SPEC],
        out_specs=[VMEM_SPEC] * len(heights),
        scratch_shapes=[
            pltpu.VMEM((rows, order), F32),
            pltpu.VMEM((depth, tile, tile), BF16),
            pltpu.SemaphoreType.DMA((depth,)),
        ],
        compiler_params=pltpu.CompilerParams(vmem_limit_bytes=34 << 20),
        cost_estimate=pl.CostEstimate(
            flops=slots * 4 * rows * tile * tile, bytes_accessed=2 * slots * tile * tile, transcendentals=0
        ),
    )(*tables, *grads, roots)


def stat_kernel(count, base, total, first_ref, second_ref, live_ref, *refs):
    grads, stat_ref = refs[:count], refs[count]
    out_ref, taken, made, in_sems, out_sems = refs[-5:]
    depth, height, tile = taken.shape
    cut = tile // height

    def place(i):
        return (base + i) // cut, lax.rem(base + i, cut) * height

    def piece(ref, i):
        slot, row = place(i)
        return ref.at[slot, pl.ds(pl.multiple_of(row, height), height), :]

    def fetch(i):
        at = lax.rem(i, depth)
        return pltpu.make_async_copy(piece(stat_ref, i), taken.at[at], in_sems.at[at])

    def store(i):
        at = lax.rem(i, depth)
        return pltpu.make_async_copy(made.at[at], piece(out_ref, i), out_sems.at[at])

    for i in range(min(depth, total)):
        fetch(i).start()

    def step(i, _):
        at = lax.rem(i, depth)
        slot, row = place(i)
        fetch(i).wait()

        @pl.when(i >= depth)
        def _():
            store(i - depth).wait()

        @pl.when(live_ref[slot] > 0)
        def _():
            left = slab(grads, first_ref[slot] * tile + row, height)
            right = slab(grads, second_ref[slot] * tile, tile)
            product = lax.dot_general(left, right, (((0,), (0,)), ((), ())), preferred_element_type=F32)
            made[at] = BETA * taken[at] + (1.0 - BETA) * product

        @pl.when(live_ref[slot] <= 0)
        def _():
            made[at] = taken[at]

        store(i).start()

        @pl.when(i + depth < total)
        def _():
            fetch(i + depth).start()

        return 0

    lax.fori_loop(0, total, step, 0)
    for i in range(max(total - depth, 0), total):
        store(i).wait()


CUT = 4


def update_stats(tables, grads, stats, base, length, done):
    slots, tile, _ = stats.shape
    rows = sum(g.shape[0] for g in grads)
    depth, height = 4, tile // CUT
    operands = [*tables, *grads, stats]
    in_specs = [SMEM_SPEC] * 3 + [VMEM_SPEC] * len(grads) + [ANY_SPEC]
    aliases = {}
    if done is not None:
        aliases = {len(operands): 0}
        operands.append(done)
        in_specs.append(ANY_SPEC)
    return pl.pallas_call(
        functools.partial(stat_kernel, len(grads), base, length),
        out_shape=jax.ShapeDtypeStruct(stats.shape, F32),
        in_specs=in_specs,
        out_specs=ANY_SPEC,
        scratch_shapes=[
            pltpu.VMEM((depth, height, tile), F32),
            pltpu.VMEM((depth, height, tile), F32),
            pltpu.SemaphoreType.DMA((depth,)),
            pltpu.SemaphoreType.DMA((depth,)),
        ],
        input_output_aliases=aliases,
        compiler_params=pltpu.CompilerParams(vmem_limit_bytes=34 << 20),
        cost_estimate=pl.CostEstimate(
            flops=length * 2 * rows * height * tile, bytes_accessed=8 * length * height * tile, transcendentals=0
        ),
    )(*operands)


def body(grad, stats, roots, tile_slot):
    width, order = grad.shape
    slots, tile, _ = stats.shape
    devices = lax.axis_size("row")
    chips, half = devices // 2, width // 2
    mine = lax.dynamic_slice_in_dim(tile_slot, lax.axis_index("row") * slots, slots)
    tables = panels_of(mine, order // tile)

    if half % 8:
        everything = lax.all_gather(grad, "row", axis=0, tiled=True)
        (sums,) = partial_sums(tables, [everything], everything.shape[:1], roots)
        new_stats = update_stats(tables, [everything], stats, 0, slots * CUT, None)
        terms = lax.all_to_all(sums, "row", split_axis=0, concat_axis=0, tiled=True)
        total = jnp.sum(terms.reshape(devices, width, order), axis=0, dtype=F32)
        return new_stats, total.astype(BF16)

    walk = chip_cycle(chips)
    forward, backward = [], []
    for here, there in zip(walk, walk[1:] + walk[:1]):
        for core in range(2):
            forward.append((2 * here + core, 2 * there + core))
            backward.append((2 * there + core, 2 * here + core))
    ahead = lambda v: lax.ppermute(v, "row", forward)
    back = lambda v: lax.ppermute(v, "row", backward)
    swap = lambda v: lax.ppermute(v, "row", [(i, i ^ 1) for i in range(devices)])

    reach = (chips - 1) // 2
    low, high = {0: grad[:half]}, {0: grad[half:]}
    chunk = {}
    for step in range(1, reach + 1):
        low[-step], high[step] = ahead(low[1 - step]), back(high[step - 1])
        high[-step], low[step] = ahead(high[1 - step]), back(low[step - 1])
        if step == 1:
            low[-1], tables = lax.optimization_barrier((low[-1], tables))
    chunk["low"], chunk["high"] = ahead(low[-reach]), back(high[reach])
    for step in range(1, reach + 1):
        halves = low[-step], high[-step], low[step], high[step]
        if step < reach:
            halves = lax.optimization_barrier((*halves, low[-reach], high[reach]))[:4]
        chunk[-step], chunk[step] = jnp.concatenate(halves[:2], 0), jnp.concatenate(halves[2:], 0)
    near = [k for step in range(reach, 0, -1) for k in (-step, step)]
    names = ["low", "high", *near, 0]
    other = {k: swap(chunk[k]) for k in near}
    other[0] = swap(grad)
    far = lax.optimization_barrier((chunk["low"], chunk["high"], *other.values()))
    chunk["low"], chunk["high"] = far[:2]
    other = dict(zip(other, far[2:]))
    other["low"], other["high"] = swap(chunk["low"]), swap(chunk["high"])
    rows = [other[k] for k in names] + [chunk[k] for k in names[:-1]] + [low[0], high[0]]
    heights = [other[k].shape[0] for k in names]
    outs = partial_sums(tables, rows, heights * 2, roots)
    other, own = dict(zip(names, outs)), dict(zip(names, outs[len(names) :]))

    here = lambda k: own[k].astype(F32) + swap(other[k]).astype(F32)
    sent = here("low").astype(BF16), here("high").astype(BF16)
    pieces = slots * CUT
    shares = [0] + [pieces - pieces * 9 * step // 32 for step in range(3, -1, -1)]
    shares = [0] * (reach - 3) + shares if reach >= 3 else [0] * (reach + 1) + [pieces]
    done = None
    for step in range(reach, -1, -1):
        low, high = back(sent[0]), ahead(sent[1])
        base, stop = shares[reach - step : reach - step + 2]
        if stop > base:
            now = lax.optimization_barrier((*tables, *sent))[: len(tables)]
            done = update_stats(now, rows, stats, base, stop - base, done)
            low, high, done = lax.optimization_barrier((low, high, done))
        low, high = low.astype(F32), high.astype(F32)
        if step == reach:
            low = jnp.pad(low, ((0, width - half), (0, 0)))
            high = jnp.pad(high, ((half, 0), (0, 0)))
        if step:
            sent = (here(-step) + low).astype(BF16), (here(step) + high).astype(BF16)
    return done, (here(0) + low + high).astype(BF16)


def solution(mesh):
    placed = (
        P(("groups", "row"), None),
        P(("groups", "row"), None, None),
        P(("groups", "row"), None, None),
        P(),
    )
    return jax.shard_map(
        body,
        mesh=mesh,
        in_specs=placed,
        out_specs=(P(("groups", "row"), None, None), P(("groups", "row"), None)),
        check_vma=False,
    )
```

```python
import functools

import jax
import jax.numpy as jnp
from jax import lax
from jax.experimental import pallas as pl
from jax.experimental.pallas import tpu as pltpu
from jax.sharding import PartitionSpec as P

BETA = 0.9
F32 = jnp.float32
BF16 = jnp.bfloat16


def panels_of(tiles, grid_len):
    number = jnp.maximum(tiles, 0)
    first = jnp.zeros_like(number)
    for row_index in range(1, grid_len):
        first = first + (number >= row_index * grid_len - row_index * (row_index - 1) // 2)
    start = first * grid_len - first * (first - 1) // 2
    return first, number - start + first, (tiles >= 0).astype(jnp.int32)


def chip_cycle(chips):
    slow = 4 if chips % 4 == 0 else 1
    fast = chips // slow
    walk = [(row, 0) for row in range(slow)]
    for step, row in enumerate(reversed(range(slow))):
        span = range(1, fast) if step % 2 == 0 else reversed(range(1, fast))
        walk += [(row, col) for col in span]
    return [row * fast + col for row, col in walk]


def slab(refs, start, size):
    columns = pl.ds(pl.multiple_of(start, size), size)
    return jnp.concatenate([ref[:, columns] for ref in refs], 0)


def part_kernel(count, first_ref, second_ref, live_ref, *refs):
    grads, early_ref, root_ref, outs = refs[:count], refs[count], refs[count + 1], refs[count + 2 : -4]
    acc, held, seen, sems = refs[-4:]
    slots, tile, _ = root_ref.shape
    early, depth = early_ref.shape[0], held.shape[0]
    panels = acc.shape[1] // tile

    def fetch(slot):
        at = lax.rem(slot, depth)
        return pltpu.make_async_copy(root_ref.at[slot], held.at[at], sems.at[at])

    for slot in range(early, min(early + depth, slots)):
        fetch(slot).start()
    for panel in range(panels):
        seen[panel] = 0

    def add(panel, part):
        columns = pl.ds(pl.multiple_of(panel * tile, tile), tile)
        acc[:, columns] = jnp.where(seen[panel] > 0, acc[:, columns], 0.0) + part.astype(BF16).astype(F32)
        seen[panel] = 1

    def use(slot, root):
        first, second = first_ref[slot], second_ref[slot]

        @pl.when(live_ref[slot] > 0)
        def _():
            rows = slab(grads, second * tile, tile)
            add(first, lax.dot_general(rows, root[...], (((1,), (1,)), ((), ())), preferred_element_type=F32))

        @pl.when((live_ref[slot] > 0) & (first != second))
        def _():
            rows = slab(grads, first * tile, tile)
            add(second, lax.dot_general(rows, root[...], (((1,), (0,)), ((), ())), preferred_element_type=F32))

    def early_step(slot, _):
        use(slot, early_ref.at[slot])
        return 0

    def step(slot, _):
        fetch(slot).wait()
        use(slot, held.at[lax.rem(slot, depth)])

        @pl.when(slot + depth < slots)
        def _():
            fetch(slot + depth).start()

        return 0

    lax.fori_loop(0, early, early_step, 0)
    lax.fori_loop(early, slots, step, 0)

    def clear(panel, _):
        @pl.when(seen[panel] == 0)
        def _():
            columns = pl.ds(pl.multiple_of(panel * tile, tile), tile)
            acc[:, columns] = jnp.zeros((acc.shape[0], tile), F32)

        return 0

    lax.fori_loop(0, panels, clear, 0)
    at = 0
    for out in outs:
        out[...] = acc[at : at + out.shape[0], :].astype(BF16)
        at += out.shape[0]


SMEM_SPEC = pl.BlockSpec(memory_space=pltpu.SMEM)
VMEM_SPEC = pl.BlockSpec(memory_space=pltpu.VMEM)
ANY_SPEC = pl.BlockSpec(memory_space=pl.ANY)
HBM_SPEC = pl.BlockSpec(memory_space=pltpu.HBM)


def early_kernel(after_ref, root_ref, early_ref, token_ref, sem):
    copy = pltpu.make_async_copy(root_ref.at[: early_ref.shape[0]], early_ref, sem)
    copy.start()
    for i in range(after_ref.shape[0]):
        token_ref[i] = after_ref[i]
    copy.wait()


def early_roots(after, roots):
    slots, tile, _ = roots.shape
    return pl.pallas_call(
        early_kernel,
        out_shape=(
            jax.ShapeDtypeStruct((min(2, slots), tile, tile), BF16),
            jax.ShapeDtypeStruct(after.shape, after.dtype),
        ),
        in_specs=[SMEM_SPEC, ANY_SPEC],
        out_specs=(VMEM_SPEC, SMEM_SPEC),
        scratch_shapes=[pltpu.SemaphoreType.DMA],
        cost_estimate=pl.CostEstimate(flops=0, bytes_accessed=4 * tile * tile, transcendentals=0),
        compiler_params=pltpu.CompilerParams(vmem_limit_bytes=40 << 20),
    )(after, roots)


def partial_sums(tables, grads, heights, roots, early):
    slots, tile, _ = roots.shape
    rows, order = sum(heights), grads[0].shape[1]
    depth = 2
    return pl.pallas_call(
        functools.partial(part_kernel, len(grads)),
        out_shape=[jax.ShapeDtypeStruct((height, order), BF16) for height in heights],
        in_specs=[SMEM_SPEC] * 3 + [VMEM_SPEC] * (len(grads) + 1) + [ANY_SPEC],
        out_specs=[VMEM_SPEC] * len(heights),
        scratch_shapes=[
            pltpu.VMEM((rows, order), F32),
            pltpu.VMEM((depth, tile, tile), BF16),
            pltpu.SMEM((order // tile,), jnp.int32),
            pltpu.SemaphoreType.DMA((depth,)),
        ],
        compiler_params=pltpu.CompilerParams(vmem_limit_bytes=34 << 20),
        cost_estimate=pl.CostEstimate(
            flops=slots * 4 * rows * tile * tile, bytes_accessed=2 * slots * tile * tile, transcendentals=0
        ),
    )(*tables, *grads, early, roots)


def stat_kernel(count, base, total, first_ref, second_ref, live_ref, *refs):
    grads, stat_ref = refs[:count], refs[count]
    out_ref, taken, made, in_sems, out_sems = refs[-5:]
    depth, height, tile = taken.shape
    cut = tile // height

    def place(i):
        return (base + i) // cut, lax.rem(base + i, cut) * height

    def piece(ref, i):
        slot, row = place(i)
        return ref.at[slot, pl.ds(pl.multiple_of(row, height), height), :]

    def fetch(i):
        at = lax.rem(i, depth)
        return pltpu.make_async_copy(piece(stat_ref, i), taken.at[at], in_sems.at[at])

    def store(i):
        at = lax.rem(i, depth)
        return pltpu.make_async_copy(made.at[at], piece(out_ref, i), out_sems.at[at])

    for i in range(min(depth, total)):
        fetch(i).start()

    def step(i, _):
        at = lax.rem(i, depth)
        slot, row = place(i)
        fetch(i).wait()

        @pl.when(i >= depth)
        def _():
            store(i - depth).wait()

        @pl.when(live_ref[slot] > 0)
        def _():
            left = slab(grads, first_ref[slot] * tile + row, height)
            right = slab(grads, second_ref[slot] * tile, tile)
            product = lax.dot_general(left, right, (((0,), (0,)), ((), ())), preferred_element_type=F32)
            made[at] = BETA * taken[at] + (1.0 - BETA) * product

        @pl.when(live_ref[slot] <= 0)
        def _():
            made[at] = taken[at]

        store(i).start()

        @pl.when(i + depth < total)
        def _():
            fetch(i + depth).start()

        return 0

    lax.fori_loop(0, total, step, 0)
    for i in range(max(total - depth, 0), total):
        store(i).wait()


CUT = 4


def update_stats(tables, grads, stats, base, length, done):
    slots, tile, _ = stats.shape
    rows = sum(g.shape[0] for g in grads)
    depth, height = 4, tile // CUT
    operands = [*tables, *grads, stats]
    in_specs = [SMEM_SPEC] * 3 + [VMEM_SPEC] * len(grads) + [ANY_SPEC]
    aliases = {}
    if done is not None:
        aliases = {len(operands): 0}
        operands.append(done)
        in_specs.append(ANY_SPEC)
    return pl.pallas_call(
        functools.partial(stat_kernel, len(grads), base, length),
        out_shape=jax.ShapeDtypeStruct(stats.shape, F32),
        in_specs=in_specs,
        out_specs=ANY_SPEC,
        scratch_shapes=[
            pltpu.VMEM((depth, height, tile), F32),
            pltpu.VMEM((depth, height, tile), F32),
            pltpu.SemaphoreType.DMA((depth,)),
            pltpu.SemaphoreType.DMA((depth,)),
        ],
        input_output_aliases=aliases,
        compiler_params=pltpu.CompilerParams(vmem_limit_bytes=34 << 20),
        cost_estimate=pl.CostEstimate(
            flops=length * 2 * rows * height * tile, bytes_accessed=8 * length * height * tile, transcendentals=0
        ),
    )(*operands)


def body(grad, stats, roots, tile_slot):
    width, order = grad.shape
    slots, tile, _ = stats.shape
    devices = lax.axis_size("row")
    chips, half = devices // 2, width // 2
    mine = lax.dynamic_slice_in_dim(tile_slot, lax.axis_index("row") * slots, slots)
    tables = panels_of(mine, order // tile)

    if half % 8:
        everything = lax.all_gather(grad, "row", axis=0, tiled=True)
        early, _ = early_roots(tables[0], roots)
        (sums,) = partial_sums(tables, [everything], everything.shape[:1], roots, early)
        new_stats = update_stats(tables, [everything], stats, 0, slots * CUT, None)
        terms = lax.all_to_all(sums, "row", split_axis=0, concat_axis=0, tiled=True)
        total = jnp.sum(terms.reshape(devices, width, order), axis=0, dtype=F32)
        return new_stats, total.astype(BF16)

    walk = chip_cycle(chips)
    forward, backward = [], []
    for here, there in zip(walk, walk[1:] + walk[:1]):
        for core in range(2):
            forward.append((2 * here + core, 2 * there + core))
            backward.append((2 * there + core, 2 * here + core))
    ahead = lambda v: lax.ppermute(v, "row", forward)
    back = lambda v: lax.ppermute(v, "row", backward)
    swap = lambda v: lax.ppermute(v, "row", [(i, i ^ 1) for i in range(devices)])

    reach = (chips - 1) // 2
    low, high = {0: grad[:half]}, {0: grad[half:]}
    chunk = {}
    for step in range(1, reach + 1):
        low[-step], high[step] = ahead(low[1 - step]), back(high[step - 1])
        high[-step], low[step] = ahead(high[1 - step]), back(low[step - 1])
        if step == 1:
            low[-1], tables = lax.optimization_barrier((low[-1], tables))
    arrived = [half_rows[sign * (reach - 1)] for half_rows in (low, high) for sign in (-1, 1)]
    late = lax.optimization_barrier((tables[0], *arrived))[0]
    early, late = early_roots(late, roots)
    low[-reach], high[reach], late = lax.optimization_barrier((low[-reach], high[reach], late))
    tables = late, *tables[1:]
    chunk["low"], chunk["high"] = ahead(low[-reach]), back(high[reach])
    other = {0: swap(grad)}

    def join(step, *after):
        halves = low[-step], high[-step], low[step], high[step]
        halves = lax.optimization_barrier((*halves, *after))[:4]
        chunk[-step], chunk[step] = jnp.concatenate(halves[:2], 0), jnp.concatenate(halves[2:], 0)
        other[-step], other[step] = swap(chunk[-step]), swap(chunk[step])

    for step in range(1, reach):
        join(step, low[-reach], high[reach])
    other["low"], other["high"] = swap(chunk["low"]), swap(chunk["high"])
    join(reach, chunk["low"], chunk["high"])
    names = ["low", "high", *[k for step in range(reach, 0, -1) for k in (-step, step)], 0]
    rows = [other[k] for k in names] + [chunk[k] for k in names[:-1]] + [low[0], high[0]]
    heights = [other[k].shape[0] for k in names]
    outs = partial_sums(tables, rows, heights * 2, roots, early)
    other, own = dict(zip(names, outs)), dict(zip(names, outs[len(names) :]))

    here = lambda k: own[k].astype(F32) + swap(other[k]).astype(F32)
    sent = here("low").astype(BF16), here("high").astype(BF16)
    pieces = slots * CUT
    shares = [0] + [pieces - pieces * 9 * step // 32 for step in range(3, -1, -1)]
    shares = [0] * (reach - 3) + shares if reach >= 3 else [0] * (reach + 1) + [pieces]
    done = None
    for step in range(reach, -1, -1):
        low, high = back(sent[0]), ahead(sent[1])
        base, stop = shares[reach - step : reach - step + 2]
        if stop > base:
            now = lax.optimization_barrier((*tables, *sent))[: len(tables)]
            done = update_stats(now, rows, stats, base, stop - base, done)
            low, high, done = lax.optimization_barrier((low, high, done))
        low, high = low.astype(F32), high.astype(F32)
        if step == reach:
            low = jnp.pad(low, ((0, width - half), (0, 0)))
            high = jnp.pad(high, ((half, 0), (0, 0)))
        if step:
            sent = (here(-step) + low).astype(BF16), (here(step) + high).astype(BF16)
    return done, (here(0) + low + high).astype(BF16)


def solution(mesh):
    placed = (
        P(("groups", "row"), None),
        P(("groups", "row"), None, None),
        P(("groups", "row"), None, None),
        P(),
    )
    return jax.shard_map(
        body,
        mesh=mesh,
        in_specs=placed,
        out_specs=(P(("groups", "row"), None, None), P(("groups", "row"), None)),
        check_vma=False,
    )
```

```python
import functools

import jax
import jax.numpy as jnp
from jax import lax
from jax.experimental import pallas as pl
from jax.experimental.pallas import tpu as pltpu
from jax.sharding import PartitionSpec as P

BETA = 0.9
F32 = jnp.float32
BF16 = jnp.bfloat16


def panels_of(tiles, grid_len):
    number = jnp.maximum(tiles, 0)
    first = jnp.zeros_like(number)
    for row_index in range(1, grid_len):
        first = first + (number >= row_index * grid_len - row_index * (row_index - 1) // 2)
    start = first * grid_len - first * (first - 1) // 2
    return first, number - start + first, (tiles >= 0).astype(jnp.int32)


def chip_cycle(chips):
    slow = 4 if chips % 4 == 0 else 1
    fast = chips // slow
    walk = [(row, 0) for row in range(slow)]
    for step, row in enumerate(reversed(range(slow))):
        span = range(1, fast) if step % 2 == 0 else reversed(range(1, fast))
        walk += [(row, col) for col in span]
    return [row * fast + col for row, col in walk]


def slab(refs, start, size):
    columns = pl.ds(pl.multiple_of(start, size), size)
    return jnp.concatenate([ref[:, columns] for ref in refs], 0)


def part_kernel(count, first_ref, second_ref, live_ref, *refs):
    grads, early_ref, root_ref, outs = refs[:count], refs[count], refs[count + 1], refs[count + 2 : -4]
    acc, held, seen, sems = refs[-4:]
    slots, tile, _ = root_ref.shape
    early, depth = early_ref.shape[0], held.shape[0]
    panels = acc.shape[1] // tile

    def fetch(slot):
        at = lax.rem(slot, depth)
        return pltpu.make_async_copy(root_ref.at[slot], held.at[at], sems.at[at])

    for slot in range(early, min(early + depth, slots)):
        fetch(slot).start()
    for panel in range(panels):
        seen[panel] = 0

    def add(panel, part):
        columns = pl.ds(pl.multiple_of(panel * tile, tile), tile)
        acc[:, columns] = jnp.where(seen[panel] > 0, acc[:, columns], 0.0) + part.astype(BF16).astype(F32)
        seen[panel] = 1

    def use(slot, root):
        first, second = first_ref[slot], second_ref[slot]

        @pl.when(live_ref[slot] > 0)
        def _():
            rows = slab(grads, second * tile, tile)
            add(first, lax.dot_general(rows, root[...], (((1,), (1,)), ((), ())), preferred_element_type=F32))

        @pl.when((live_ref[slot] > 0) & (first != second))
        def _():
            rows = slab(grads, first * tile, tile)
            add(second, lax.dot_general(rows, root[...], (((1,), (0,)), ((), ())), preferred_element_type=F32))

    def early_step(slot, _):
        use(slot, early_ref.at[slot])
        return 0

    def step(slot, _):
        fetch(slot).wait()
        use(slot, held.at[lax.rem(slot, depth)])

        @pl.when(slot + depth < slots)
        def _():
            fetch(slot + depth).start()

        return 0

    lax.fori_loop(0, early, early_step, 0)
    lax.fori_loop(early, slots, step, 0)

    def clear(panel, _):
        @pl.when(seen[panel] == 0)
        def _():
            columns = pl.ds(pl.multiple_of(panel * tile, tile), tile)
            acc[:, columns] = jnp.zeros((acc.shape[0], tile), F32)

        return 0

    lax.fori_loop(0, panels, clear, 0)
    at = 0
    for out in outs:
        out[...] = acc[at : at + out.shape[0], :].astype(BF16)
        at += out.shape[0]


SMEM_SPEC = pl.BlockSpec(memory_space=pltpu.SMEM)
VMEM_SPEC = pl.BlockSpec(memory_space=pltpu.VMEM)
ANY_SPEC = pl.BlockSpec(memory_space=pl.ANY)
HBM_SPEC = pl.BlockSpec(memory_space=pltpu.HBM)


def early_kernel(after_ref, root_ref, early_ref, token_ref, sem):
    copy = pltpu.make_async_copy(root_ref.at[: early_ref.shape[0]], early_ref, sem)
    copy.start()
    for i in range(after_ref.shape[0]):
        token_ref[i] = after_ref[i]
    copy.wait()


def early_roots(after, roots):
    slots, tile, _ = roots.shape
    return pl.pallas_call(
        early_kernel,
        out_shape=(
            jax.ShapeDtypeStruct((min(2, slots), tile, tile), BF16),
            jax.ShapeDtypeStruct(after.shape, after.dtype),
        ),
        in_specs=[SMEM_SPEC, ANY_SPEC],
        out_specs=(VMEM_SPEC, SMEM_SPEC),
        scratch_shapes=[pltpu.SemaphoreType.DMA],
        cost_estimate=pl.CostEstimate(flops=0, bytes_accessed=4 * tile * tile, transcendentals=0),
        compiler_params=pltpu.CompilerParams(vmem_limit_bytes=40 << 20),
    )(after, roots)


def partial_sums(tables, grads, heights, roots, early):
    slots, tile, _ = roots.shape
    rows, order = sum(heights), grads[0].shape[1]
    depth = 2
    return pl.pallas_call(
        functools.partial(part_kernel, len(grads)),
        out_shape=[jax.ShapeDtypeStruct((height, order), BF16) for height in heights],
        in_specs=[SMEM_SPEC] * 3 + [VMEM_SPEC] * (len(grads) + 1) + [ANY_SPEC],
        out_specs=[VMEM_SPEC] * len(heights),
        scratch_shapes=[
            pltpu.VMEM((rows, order), F32),
            pltpu.VMEM((depth, tile, tile), BF16),
            pltpu.SMEM((order // tile,), jnp.int32),
            pltpu.SemaphoreType.DMA((depth,)),
        ],
        compiler_params=pltpu.CompilerParams(vmem_limit_bytes=34 << 20),
        cost_estimate=pl.CostEstimate(
            flops=slots * 4 * rows * tile * tile, bytes_accessed=2 * slots * tile * tile, transcendentals=0
        ),
    )(*tables, *grads, early, roots)


def stat_kernel(count, base, total, first_ref, second_ref, live_ref, *refs):
    grads, stat_ref = refs[:count], refs[count]
    out_ref, taken, made, in_sems, out_sems = refs[-5:]
    depth, height, tile = taken.shape
    cut = tile // height

    def place(i):
        return (base + i) // cut, lax.rem(base + i, cut) * height

    def piece(ref, i):
        slot, row = place(i)
        return ref.at[slot, pl.ds(pl.multiple_of(row, height), height), :]

    def fetch(i):
        at = lax.rem(i, depth)
        return pltpu.make_async_copy(piece(stat_ref, i), taken.at[at], in_sems.at[at])

    def store(i):
        at = lax.rem(i, depth)
        return pltpu.make_async_copy(made.at[at], piece(out_ref, i), out_sems.at[at])

    for i in range(min(depth, total)):
        fetch(i).start()

    def step(i, _):
        at = lax.rem(i, depth)
        slot, row = place(i)
        fetch(i).wait()

        @pl.when(i >= depth)
        def _():
            store(i - depth).wait()

        @pl.when(live_ref[slot] > 0)
        def _():
            left = slab(grads, first_ref[slot] * tile + row, height)
            right = slab(grads, second_ref[slot] * tile, tile)
            product = lax.dot_general(left, right, (((0,), (0,)), ((), ())), preferred_element_type=F32)
            made[at] = BETA * taken[at] + (1.0 - BETA) * product

        @pl.when(live_ref[slot] <= 0)
        def _():
            made[at] = taken[at]

        store(i).start()

        @pl.when(i + depth < total)
        def _():
            fetch(i + depth).start()

        return 0

    lax.fori_loop(0, total, step, 0)
    for i in range(max(total - depth, 0), total):
        store(i).wait()


CUT = 4


def update_stats(tables, grads, stats, base, length, done):
    slots, tile, _ = stats.shape
    rows = sum(g.shape[0] for g in grads)
    depth, height = 4, tile // CUT
    operands = [*tables, *grads, stats]
    in_specs = [SMEM_SPEC] * 3 + [VMEM_SPEC] * len(grads) + [ANY_SPEC]
    aliases = {}
    if done is not None:
        aliases = {len(operands): 0}
        operands.append(done)
        in_specs.append(ANY_SPEC)
    return pl.pallas_call(
        functools.partial(stat_kernel, len(grads), base, length),
        out_shape=jax.ShapeDtypeStruct(stats.shape, F32),
        in_specs=in_specs,
        out_specs=ANY_SPEC,
        scratch_shapes=[
            pltpu.VMEM((depth, height, tile), F32),
            pltpu.VMEM((depth, height, tile), F32),
            pltpu.SemaphoreType.DMA((depth,)),
            pltpu.SemaphoreType.DMA((depth,)),
        ],
        input_output_aliases=aliases,
        compiler_params=pltpu.CompilerParams(vmem_limit_bytes=34 << 20),
        cost_estimate=pl.CostEstimate(
            flops=length * 2 * rows * height * tile, bytes_accessed=8 * length * height * tile, transcendentals=0
        ),
    )(*operands)


def body(grad, stats, roots, tile_slot):
    width, order = grad.shape
    slots, tile, _ = stats.shape
    devices = lax.axis_size("row")
    chips, half = devices // 2, width // 2
    mine = lax.dynamic_slice_in_dim(tile_slot, lax.axis_index("row") * slots, slots)
    tables = panels_of(mine, order // tile)

    if half % 8:
        everything = lax.all_gather(grad, "row", axis=0, tiled=True)
        early, _ = early_roots(tables[0], roots)
        (sums,) = partial_sums(tables, [everything], everything.shape[:1], roots, early)
        new_stats = update_stats(tables, [everything], stats, 0, slots * CUT, None)
        terms = lax.all_to_all(sums, "row", split_axis=0, concat_axis=0, tiled=True)
        total = jnp.sum(terms.reshape(devices, width, order), axis=0, dtype=F32)
        return new_stats, total.astype(BF16)

    walk = chip_cycle(chips)
    forward, backward = [], []
    for here, there in zip(walk, walk[1:] + walk[:1]):
        for core in range(2):
            forward.append((2 * here + core, 2 * there + core))
            backward.append((2 * there + core, 2 * here + core))
    ahead = lambda v: lax.ppermute(v, "row", forward)
    back = lambda v: lax.ppermute(v, "row", backward)
    swap = lambda v: lax.ppermute(v, "row", [(i, i ^ 1) for i in range(devices)])

    reach = (chips - 1) // 2
    low, high = {0: grad[:half]}, {0: grad[half:]}
    chunk = {}
    for step in range(1, reach + 1):
        low[-step], high[step] = ahead(low[1 - step]), back(high[step - 1])
        high[-step], low[step] = ahead(high[1 - step]), back(low[step - 1])
        if step == 1:
            low[-1], tables = lax.optimization_barrier((low[-1], tables))
    arrived = [half_rows[sign * (reach - 1)] for half_rows in (low, high) for sign in (-1, 1)]
    late = lax.optimization_barrier((tables[0], *arrived))[0]
    early, late = early_roots(late, roots)
    low[-reach], high[reach], late = lax.optimization_barrier((low[-reach], high[reach], late))
    tables = late, *tables[1:]
    chunk["low"], chunk["high"] = ahead(low[-reach]), back(high[reach])
    other = {0: swap(grad)}

    def join(step, *after):
        halves = low[-step], high[-step], low[step], high[step]
        if after:
            halves = lax.optimization_barrier((*halves, *after))[:4]
        chunk[-step], chunk[step] = jnp.concatenate(halves[:2], 0), jnp.concatenate(halves[2:], 0)
        other[-step], other[step] = swap(chunk[-step]), swap(chunk[step])

    for step in range(1, reach):
        join(step, low[-reach], high[reach])
    join(reach)
    last = lax.optimization_barrier((chunk["low"], chunk["high"], other[-reach], other[reach]))
    chunk["low"], chunk["high"], other[-reach], other[reach] = last
    other["low"], other["high"] = swap(chunk["low"]), swap(chunk["high"])
    names = ["low", "high", *[k for step in range(reach, 0, -1) for k in (-step, step)], 0]
    rows = [other[k] for k in names] + [chunk[k] for k in names[:-1]] + [low[0], high[0]]
    heights = [other[k].shape[0] for k in names]
    outs = partial_sums(tables, rows, heights * 2, roots, early)
    other, own = dict(zip(names, outs)), dict(zip(names, outs[len(names) :]))

    here = lambda k: own[k].astype(F32) + swap(other[k]).astype(F32)
    sent = here("low").astype(BF16), here("high").astype(BF16)
    pieces = slots * CUT
    shares = [0] + [pieces - pieces * 9 * step // 32 for step in range(3, -1, -1)]
    shares = [0] * (reach - 3) + shares if reach >= 3 else [0] * (reach + 1) + [pieces]
    done = None
    for step in range(reach, -1, -1):
        low, high = back(sent[0]), ahead(sent[1])
        base, stop = shares[reach - step : reach - step + 2]
        if stop > base:
            now = lax.optimization_barrier((*tables, *sent))[: len(tables)]
            done = update_stats(now, rows, stats, base, stop - base, done)
            low, high, done = lax.optimization_barrier((low, high, done))
        low, high = low.astype(F32), high.astype(F32)
        if step == reach:
            low = jnp.pad(low, ((0, width - half), (0, 0)))
            high = jnp.pad(high, ((half, 0), (0, 0)))
        if step:
            sent = (here(-step) + low).astype(BF16), (here(step) + high).astype(BF16)
    return done, (here(0) + low + high).astype(BF16)


def solution(mesh):
    placed = (
        P(("groups", "row"), None),
        P(("groups", "row"), None, None),
        P(("groups", "row"), None, None),
        P(),
    )
    return jax.shard_map(
        body,
        mesh=mesh,
        in_specs=placed,
        out_specs=(P(("groups", "row"), None, None), P(("groups", "row"), None)),
        check_vma=False,
    )
```

```python
import functools

import jax
import jax.numpy as jnp
from jax import lax
from jax.experimental import pallas as pl
from jax.experimental.pallas import tpu as pltpu
from jax.sharding import PartitionSpec as P

BETA = 0.9
F32 = jnp.float32
BF16 = jnp.bfloat16


def panels_of(tiles, grid_len):
    number = jnp.maximum(tiles, 0)
    first = jnp.zeros_like(number)
    for row_index in range(1, grid_len):
        first = first + (number >= row_index * grid_len - row_index * (row_index - 1) // 2)
    start = first * grid_len - first * (first - 1) // 2
    return first, number - start + first, (tiles >= 0).astype(jnp.int32)


def chip_cycle(chips):
    slow = 4 if chips % 4 == 0 else 1
    fast = chips // slow
    walk = [(row, 0) for row in range(slow)]
    for step, row in enumerate(reversed(range(slow))):
        span = range(1, fast) if step % 2 == 0 else reversed(range(1, fast))
        walk += [(row, col) for col in span]
    return [row * fast + col for row, col in walk]


def slab(refs, start, size):
    columns = pl.ds(pl.multiple_of(start, size), size)
    return jnp.concatenate([ref[:, columns] for ref in refs], 0)


def part_kernel(count, first_ref, second_ref, live_ref, *refs):
    grads, early_ref, root_ref, outs = refs[:count], refs[count], refs[count + 1], refs[count + 2 : -4]
    acc, held, seen, sems = refs[-4:]
    slots, tile, _ = root_ref.shape
    early, depth = early_ref.shape[0], held.shape[0]
    panels = acc.shape[1] // tile

    def fetch(slot):
        at = lax.rem(slot, depth)
        return pltpu.make_async_copy(root_ref.at[slot], held.at[at], sems.at[at])

    for slot in range(early, min(early + depth, slots)):
        fetch(slot).start()
    for panel in range(panels):
        seen[panel] = 0

    def add(panel, part):
        columns = pl.ds(pl.multiple_of(panel * tile, tile), tile)
        acc[:, columns] = jnp.where(seen[panel] > 0, acc[:, columns], 0.0) + part.astype(BF16).astype(F32)
        seen[panel] = 1

    def use(slot, root):
        first, second = first_ref[slot], second_ref[slot]

        @pl.when(live_ref[slot] > 0)
        def _():
            rows = slab(grads, second * tile, tile)
            part = lax.dot_general(rows, root[...], (((1,), (1,)), ((), ())), preferred_element_type=F32)
            rows = slab(grads, first * tile, tile)
            other = lax.dot_general(rows, root[...], (((1,), (0,)), ((), ())), preferred_element_type=F32)
            add(first, part)
            add(second, jnp.where(first != second, other, 0.0))

    def early_step(slot, _):
        use(slot, early_ref.at[slot])
        return 0

    def step(slot, _):
        fetch(slot).wait()
        use(slot, held.at[lax.rem(slot, depth)])

        @pl.when(slot + depth < slots)
        def _():
            fetch(slot + depth).start()

        return 0

    lax.fori_loop(0, early, early_step, 0)
    lax.fori_loop(early, slots, step, 0)

    def clear(panel, _):
        @pl.when(seen[panel] == 0)
        def _():
            columns = pl.ds(pl.multiple_of(panel * tile, tile), tile)
            acc[:, columns] = jnp.zeros((acc.shape[0], tile), F32)

        return 0

    lax.fori_loop(0, panels, clear, 0)
    at = 0
    for out in outs:
        out[...] = acc[at : at + out.shape[0], :].astype(BF16)
        at += out.shape[0]


SMEM_SPEC = pl.BlockSpec(memory_space=pltpu.SMEM)
VMEM_SPEC = pl.BlockSpec(memory_space=pltpu.VMEM)
ANY_SPEC = pl.BlockSpec(memory_space=pl.ANY)
HBM_SPEC = pl.BlockSpec(memory_space=pltpu.HBM)


def early_kernel(after_ref, root_ref, early_ref, token_ref, sem):
    copy = pltpu.make_async_copy(root_ref.at[: early_ref.shape[0]], early_ref, sem)
    copy.start()
    for i in range(after_ref.shape[0]):
        token_ref[i] = after_ref[i]
    copy.wait()


def early_roots(after, roots):
    slots, tile, _ = roots.shape
    return pl.pallas_call(
        early_kernel,
        out_shape=(
            jax.ShapeDtypeStruct((min(2, slots), tile, tile), BF16),
            jax.ShapeDtypeStruct(after.shape, after.dtype),
        ),
        in_specs=[SMEM_SPEC, ANY_SPEC],
        out_specs=(VMEM_SPEC, SMEM_SPEC),
        scratch_shapes=[pltpu.SemaphoreType.DMA],
        cost_estimate=pl.CostEstimate(flops=0, bytes_accessed=4 * tile * tile, transcendentals=0),
        compiler_params=pltpu.CompilerParams(vmem_limit_bytes=40 << 20),
    )(after, roots)


def partial_sums(tables, grads, heights, roots, early):
    slots, tile, _ = roots.shape
    rows, order = sum(heights), grads[0].shape[1]
    depth = 2
    return pl.pallas_call(
        functools.partial(part_kernel, len(grads)),
        out_shape=[jax.ShapeDtypeStruct((height, order), BF16) for height in heights],
        in_specs=[SMEM_SPEC] * 3 + [VMEM_SPEC] * (len(grads) + 1) + [ANY_SPEC],
        out_specs=[VMEM_SPEC] * len(heights),
        scratch_shapes=[
            pltpu.VMEM((rows, order), F32),
            pltpu.VMEM((depth, tile, tile), BF16),
            pltpu.SMEM((order // tile,), jnp.int32),
            pltpu.SemaphoreType.DMA((depth,)),
        ],
        compiler_params=pltpu.CompilerParams(vmem_limit_bytes=34 << 20),
        cost_estimate=pl.CostEstimate(
            flops=slots * 4 * rows * tile * tile, bytes_accessed=2 * slots * tile * tile, transcendentals=0
        ),
    )(*tables, *grads, early, roots)


def stat_kernel(count, base, total, first_ref, second_ref, live_ref, *refs):
    grads, stat_ref = refs[:count], refs[count]
    out_ref, taken, made, in_sems, out_sems = refs[-5:]
    depth, height, tile = taken.shape
    cut = tile // height

    def place(i):
        return (base + i) // cut, lax.rem(base + i, cut) * height

    def piece(ref, i):
        slot, row = place(i)
        return ref.at[slot, pl.ds(pl.multiple_of(row, height), height), :]

    def fetch(i):
        at = lax.rem(i, depth)
        return pltpu.make_async_copy(piece(stat_ref, i), taken.at[at], in_sems.at[at])

    def store(i):
        at = lax.rem(i, depth)
        return pltpu.make_async_copy(made.at[at], piece(out_ref, i), out_sems.at[at])

    for i in range(min(depth, total)):
        fetch(i).start()

    def step(i, _):
        at = lax.rem(i, depth)
        slot, row = place(i)
        fetch(i).wait()

        @pl.when(i >= depth)
        def _():
            store(i - depth).wait()

        @pl.when(live_ref[slot] > 0)
        def _():
            left = slab(grads, first_ref[slot] * tile + row, height)
            right = slab(grads, second_ref[slot] * tile, tile)
            product = lax.dot_general(left, right, (((0,), (0,)), ((), ())), preferred_element_type=F32)
            made[at] = BETA * taken[at] + (1.0 - BETA) * product

        @pl.when(live_ref[slot] <= 0)
        def _():
            made[at] = taken[at]

        store(i).start()

        @pl.when(i + depth < total)
        def _():
            fetch(i + depth).start()

        return 0

    lax.fori_loop(0, total, step, 0)
    for i in range(max(total - depth, 0), total):
        store(i).wait()


CUT = 4


def update_stats(tables, grads, stats, base, length, done):
    slots, tile, _ = stats.shape
    rows = sum(g.shape[0] for g in grads)
    depth, height = 4, tile // CUT
    operands = [*tables, *grads, stats]
    in_specs = [SMEM_SPEC] * 3 + [VMEM_SPEC] * len(grads) + [ANY_SPEC]
    aliases = {}
    if done is not None:
        aliases = {len(operands): 0}
        operands.append(done)
        in_specs.append(ANY_SPEC)
    return pl.pallas_call(
        functools.partial(stat_kernel, len(grads), base, length),
        out_shape=jax.ShapeDtypeStruct(stats.shape, F32),
        in_specs=in_specs,
        out_specs=ANY_SPEC,
        scratch_shapes=[
            pltpu.VMEM((depth, height, tile), F32),
            pltpu.VMEM((depth, height, tile), F32),
            pltpu.SemaphoreType.DMA((depth,)),
            pltpu.SemaphoreType.DMA((depth,)),
        ],
        input_output_aliases=aliases,
        compiler_params=pltpu.CompilerParams(vmem_limit_bytes=34 << 20),
        cost_estimate=pl.CostEstimate(
            flops=length * 2 * rows * height * tile, bytes_accessed=8 * length * height * tile, transcendentals=0
        ),
    )(*operands)


def body(grad, stats, roots, tile_slot):
    width, order = grad.shape
    slots, tile, _ = stats.shape
    devices = lax.axis_size("row")
    chips, half = devices // 2, width // 2
    mine = lax.dynamic_slice_in_dim(tile_slot, lax.axis_index("row") * slots, slots)
    tables = panels_of(mine, order // tile)

    if half % 8:
        everything = lax.all_gather(grad, "row", axis=0, tiled=True)
        early, _ = early_roots(tables[0], roots)
        (sums,) = partial_sums(tables, [everything], everything.shape[:1], roots, early)
        new_stats = update_stats(tables, [everything], stats, 0, slots * CUT, None)
        terms = lax.all_to_all(sums, "row", split_axis=0, concat_axis=0, tiled=True)
        total = jnp.sum(terms.reshape(devices, width, order), axis=0, dtype=F32)
        return new_stats, total.astype(BF16)

    walk = chip_cycle(chips)
    forward, backward = [], []
    for here, there in zip(walk, walk[1:] + walk[:1]):
        for core in range(2):
            forward.append((2 * here + core, 2 * there + core))
            backward.append((2 * there + core, 2 * here + core))
    ahead = lambda v: lax.ppermute(v, "row", forward)
    back = lambda v: lax.ppermute(v, "row", backward)
    swap = lambda v: lax.ppermute(v, "row", [(i, i ^ 1) for i in range(devices)])

    reach = (chips - 1) // 2
    low, high = {0: grad[:half]}, {0: grad[half:]}
    chunk = {}
    for step in range(1, reach + 1):
        low[-step], high[step] = ahead(low[1 - step]), back(high[step - 1])
        high[-step], low[step] = ahead(high[1 - step]), back(low[step - 1])
        if step == 1:
            low[-1], tables = lax.optimization_barrier((low[-1], tables))
    arrived = [half_rows[sign * (reach - 1)] for half_rows in (low, high) for sign in (-1, 1)]
    late = lax.optimization_barrier((tables[0], *arrived))[0]
    early, late = early_roots(late, roots)
    low[-reach], high[reach], late = lax.optimization_barrier((low[-reach], high[reach], late))
    tables = late, *tables[1:]
    chunk["low"], chunk["high"] = ahead(low[-reach]), back(high[reach])
    other = {0: swap(grad)}

    def join(step, *after):
        halves = low[-step], high[-step], low[step], high[step]
        if after:
            halves = lax.optimization_barrier((*halves, *after))[:4]
        chunk[-step], chunk[step] = jnp.concatenate(halves[:2], 0), jnp.concatenate(halves[2:], 0)
        other[-step], other[step] = swap(chunk[-step]), swap(chunk[step])

    for step in range(1, reach):
        join(step, low[-reach], high[reach])
    join(reach)
    last = lax.optimization_barrier((chunk["low"], chunk["high"], other[-reach], other[reach]))
    chunk["low"], chunk["high"], other[-reach], other[reach] = last
    other["low"], other["high"] = swap(chunk["low"]), swap(chunk["high"])
    names = ["low", "high", *[k for step in range(reach, 0, -1) for k in (-step, step)], 0]
    rows = [other[k] for k in names] + [chunk[k] for k in names[:-1]] + [low[0], high[0]]
    heights = [other[k].shape[0] for k in names]
    outs = partial_sums(tables, rows, heights * 2, roots, early)
    other, own = dict(zip(names, outs)), dict(zip(names, outs[len(names) :]))

    here = lambda k: own[k].astype(F32) + swap(other[k]).astype(F32)
    sent = here("low").astype(BF16), here("high").astype(BF16)
    pieces = slots * CUT
    shares = [0] + [pieces - pieces * 9 * step // 32 for step in range(3, -1, -1)]
    shares = [0] * (reach - 3) + shares if reach >= 3 else [0] * (reach + 1) + [pieces]
    done = None
    for step in range(reach, -1, -1):
        low, high = back(sent[0]), ahead(sent[1])
        base, stop = shares[reach - step : reach - step + 2]
        if stop > base:
            now = lax.optimization_barrier((*tables, *sent))[: len(tables)]
            done = update_stats(now, rows, stats, base, stop - base, done)
            low, high, done = lax.optimization_barrier((low, high, done))
        low, high = low.astype(F32), high.astype(F32)
        if step == reach:
            low = jnp.pad(low, ((0, width - half), (0, 0)))
            high = jnp.pad(high, ((half, 0), (0, 0)))
        if step:
            sent = (here(-step) + low).astype(BF16), (here(step) + high).astype(BF16)
    return done, (here(0) + low + high).astype(BF16)


def solution(mesh):
    placed = (
        P(("groups", "row"), None),
        P(("groups", "row"), None, None),
        P(("groups", "row"), None, None),
        P(),
    )
    return jax.shard_map(
        body,
        mesh=mesh,
        in_specs=placed,
        out_specs=(P(("groups", "row"), None, None), P(("groups", "row"), None)),
        check_vma=False,
    )
```

```python
import functools

import jax
import jax.numpy as jnp
from jax import lax
from jax.experimental import pallas as pl
from jax.experimental.pallas import tpu as pltpu
from jax.sharding import PartitionSpec as P

BETA = 0.9
F32 = jnp.float32
BF16 = jnp.bfloat16


def panels_of(tiles, grid_len):
    number = jnp.maximum(tiles, 0)
    first = jnp.zeros_like(number)
    for row_index in range(1, grid_len):
        first = first + (number >= row_index * grid_len - row_index * (row_index - 1) // 2)
    start = first * grid_len - first * (first - 1) // 2
    return first, number - start + first, (tiles >= 0).astype(jnp.int32)


def chip_cycle(chips):
    slow = 4 if chips % 4 == 0 else 1
    fast = chips // slow
    walk = [(row, 0) for row in range(slow)]
    for step, row in enumerate(reversed(range(slow))):
        span = range(1, fast) if step % 2 == 0 else reversed(range(1, fast))
        walk += [(row, col) for col in span]
    return [row * fast + col for row, col in walk]


def slab(refs, start, size):
    columns = pl.ds(pl.multiple_of(start, size), size)
    return jnp.concatenate([ref[:, columns] for ref in refs], 0)


def part_kernel(count, first_ref, second_ref, live_ref, *refs):
    grads, early_ref, root_ref, outs = refs[:count], refs[count], refs[count + 1], refs[count + 2 : -4]
    acc, held, seen, sems = refs[-4:]
    slots, tile, _ = root_ref.shape
    early, depth = early_ref.shape[0], held.shape[0]
    panels = acc.shape[1] // tile

    def fetch(slot):
        at = lax.rem(slot, depth)
        return pltpu.make_async_copy(root_ref.at[slot], held.at[at], sems.at[at])

    for slot in range(early, min(early + depth, slots)):
        fetch(slot).start()
    for panel in range(panels):
        seen[panel] = 0

    def add(panel, part):
        columns = pl.ds(pl.multiple_of(panel * tile, tile), tile)
        acc[:, columns] = jnp.where(seen[panel] > 0, acc[:, columns], 0.0) + part.astype(BF16).astype(F32)
        seen[panel] = 1

    def use(slot, root):
        first, second = first_ref[slot], second_ref[slot]

        @pl.when(live_ref[slot] > 0)
        def _():
            rows = slab(grads, second * tile, tile)
            part = lax.dot_general(rows, root[...], (((1,), (1,)), ((), ())), preferred_element_type=F32)
            rows = slab(grads, first * tile, tile)
            other = lax.dot_general(rows, root[...], (((1,), (0,)), ((), ())), preferred_element_type=F32)
            add(first, part)
            add(second, jnp.where(first != second, other, 0.0))

    def early_step(slot, _):
        use(slot, early_ref.at[slot])
        return 0

    def step(slot, _):
        fetch(slot).wait()
        use(slot, held.at[lax.rem(slot, depth)])

        @pl.when(slot + depth < slots)
        def _():
            fetch(slot + depth).start()

        return 0

    lax.fori_loop(0, early, early_step, 0)
    lax.fori_loop(early, slots, step, 0)

    def clear(panel, _):
        @pl.when(seen[panel] == 0)
        def _():
            columns = pl.ds(pl.multiple_of(panel * tile, tile), tile)
            acc[:, columns] = jnp.zeros((acc.shape[0], tile), F32)

        return 0

    lax.fori_loop(0, panels, clear, 0)
    at = 0
    for out in outs:
        out[...] = acc[at : at + out.shape[0], :].astype(BF16)
        at += out.shape[0]


SMEM_SPEC = pl.BlockSpec(memory_space=pltpu.SMEM)
VMEM_SPEC = pl.BlockSpec(memory_space=pltpu.VMEM)
ANY_SPEC = pl.BlockSpec(memory_space=pl.ANY)
HBM_SPEC = pl.BlockSpec(memory_space=pltpu.HBM)


def early_kernel(after_ref, root_ref, early_ref, token_ref, sem):
    copy = pltpu.make_async_copy(root_ref.at[: early_ref.shape[0]], early_ref, sem)
    copy.start()
    for i in range(after_ref.shape[0]):
        token_ref[i] = after_ref[i]
    copy.wait()


def early_roots(after, roots):
    slots, tile, _ = roots.shape
    return pl.pallas_call(
        early_kernel,
        out_shape=(
            jax.ShapeDtypeStruct((min(2, slots), tile, tile), BF16),
            jax.ShapeDtypeStruct(after.shape, after.dtype),
        ),
        in_specs=[SMEM_SPEC, ANY_SPEC],
        out_specs=(VMEM_SPEC, SMEM_SPEC),
        scratch_shapes=[pltpu.SemaphoreType.DMA],
        cost_estimate=pl.CostEstimate(flops=0, bytes_accessed=4 * tile * tile, transcendentals=0),
        compiler_params=pltpu.CompilerParams(vmem_limit_bytes=40 << 20),
    )(after, roots)


def partial_sums(tables, grads, heights, roots, early):
    slots, tile, _ = roots.shape
    rows, order = sum(heights), grads[0].shape[1]
    depth = 2
    return pl.pallas_call(
        functools.partial(part_kernel, len(grads)),
        out_shape=[jax.ShapeDtypeStruct((height, order), BF16) for height in heights],
        in_specs=[SMEM_SPEC] * 3 + [VMEM_SPEC] * (len(grads) + 1) + [ANY_SPEC],
        out_specs=[VMEM_SPEC] * len(heights),
        scratch_shapes=[
            pltpu.VMEM((rows, order), F32),
            pltpu.VMEM((depth, tile, tile), BF16),
            pltpu.SMEM((order // tile,), jnp.int32),
            pltpu.SemaphoreType.DMA((depth,)),
        ],
        compiler_params=pltpu.CompilerParams(vmem_limit_bytes=34 << 20),
        cost_estimate=pl.CostEstimate(
            flops=slots * 4 * rows * tile * tile, bytes_accessed=2 * slots * tile * tile, transcendentals=0
        ),
    )(*tables, *grads, early, roots)


def stat_kernel(count, base, total, first_ref, second_ref, live_ref, *refs):
    grads, stat_ref = refs[:count], refs[count]
    out_ref, taken, made, in_sems, out_sems = refs[-5:]
    depth, height, tile = taken.shape
    cut = tile // height

    def place(i):
        return (base + i) // cut, lax.rem(base + i, cut) * height

    def piece(ref, i):
        slot, row = place(i)
        return ref.at[slot, pl.ds(pl.multiple_of(row, height), height), :]

    def fetch(i):
        at = lax.rem(i, depth)
        return pltpu.make_async_copy(piece(stat_ref, i), taken.at[at], in_sems.at[at])

    def store(i):
        at = lax.rem(i, depth)
        return pltpu.make_async_copy(made.at[at], piece(out_ref, i), out_sems.at[at])

    for i in range(min(depth, total)):
        fetch(i).start()

    def step(i, _):
        at = lax.rem(i, depth)
        slot, row = place(i)
        fetch(i).wait()

        @pl.when(i >= depth)
        def _():
            store(i - depth).wait()

        @pl.when(live_ref[slot] > 0)
        def _():
            left = slab(grads, first_ref[slot] * tile + row, height)
            right = slab(grads, second_ref[slot] * tile, tile)
            product = lax.dot_general(left, right, (((0,), (0,)), ((), ())), preferred_element_type=F32)
            made[at] = BETA * taken[at] + (1.0 - BETA) * product

        @pl.when(live_ref[slot] <= 0)
        def _():
            made[at] = taken[at]

        store(i).start()

        @pl.when(i + depth < total)
        def _():
            fetch(i + depth).start()

        return 0

    lax.fori_loop(0, total, step, 0)
    for i in range(max(total - depth, 0), total):
        store(i).wait()


CUT = 4


def update_stats(tables, grads, stats, base, length, done):
    slots, tile, _ = stats.shape
    rows = sum(g.shape[0] for g in grads)
    depth, height = 4, tile // CUT
    operands = [*tables, *grads, stats]
    in_specs = [SMEM_SPEC] * 3 + [VMEM_SPEC] * len(grads) + [ANY_SPEC]
    aliases = {}
    if done is not None:
        aliases = {len(operands): 0}
        operands.append(done)
        in_specs.append(ANY_SPEC)
    return pl.pallas_call(
        functools.partial(stat_kernel, len(grads), base, length),
        out_shape=jax.ShapeDtypeStruct(stats.shape, F32),
        in_specs=in_specs,
        out_specs=ANY_SPEC,
        scratch_shapes=[
            pltpu.VMEM((depth, height, tile), F32),
            pltpu.VMEM((depth, height, tile), F32),
            pltpu.SemaphoreType.DMA((depth,)),
            pltpu.SemaphoreType.DMA((depth,)),
        ],
        input_output_aliases=aliases,
        compiler_params=pltpu.CompilerParams(vmem_limit_bytes=34 << 20),
        cost_estimate=pl.CostEstimate(
            flops=length * 2 * rows * height * tile, bytes_accessed=8 * length * height * tile, transcendentals=0
        ),
    )(*operands)


def body(grad, stats, roots, tile_slot):
    width, order = grad.shape
    slots, tile, _ = stats.shape
    devices = lax.axis_size("row")
    chips, half = devices // 2, width // 2
    mine = lax.dynamic_slice_in_dim(tile_slot, lax.axis_index("row") * slots, slots)
    tables = panels_of(mine, order // tile)

    if half % 8:
        everything = lax.all_gather(grad, "row", axis=0, tiled=True)
        early, _ = early_roots(tables[0], roots)
        (sums,) = partial_sums(tables, [everything], everything.shape[:1], roots, early)
        new_stats = update_stats(tables, [everything], stats, 0, slots * CUT, None)
        terms = lax.all_to_all(sums, "row", split_axis=0, concat_axis=0, tiled=True)
        total = jnp.sum(terms.reshape(devices, width, order), axis=0, dtype=F32)
        return new_stats, total.astype(BF16)

    walk = chip_cycle(chips)
    forward, backward = [], []
    for here, there in zip(walk, walk[1:] + walk[:1]):
        for core in range(2):
            forward.append((2 * here + core, 2 * there + core))
            backward.append((2 * there + core, 2 * here + core))
    ahead = lambda v: lax.ppermute(v, "row", forward)
    back = lambda v: lax.ppermute(v, "row", backward)
    swap = lambda v: lax.ppermute(v, "row", [(i, i ^ 1) for i in range(devices)])

    reach = (chips - 1) // 2
    low, high = {0: grad[:half]}, {0: grad[half:]}
    chunk = {}
    for step in range(1, reach + 1):
        low[-step], high[step] = ahead(low[1 - step]), back(high[step - 1])
        high[-step], low[step] = ahead(high[1 - step]), back(low[step - 1])
        if step == 1:
            low[-1], tables = lax.optimization_barrier((low[-1], tables))
    arrived = [half_rows[sign * (reach - 1)] for half_rows in (low, high) for sign in (-1, 1)]
    late = lax.optimization_barrier((tables[0], *arrived))[0]
    early, late = early_roots(late, roots)
    low[-reach], high[reach], late = lax.optimization_barrier((low[-reach], high[reach], late))
    tables = late, *tables[1:]
    chunk["low"], chunk["high"] = ahead(low[-reach]), back(high[reach])
    other = {0: swap(grad)}

    def join(step, *after):
        halves = low[-step], high[-step], low[step], high[step]
        if after:
            halves = lax.optimization_barrier((*halves, *after))[:4]
        chunk[-step], chunk[step] = jnp.concatenate(halves[:2], 0), jnp.concatenate(halves[2:], 0)
        other[-step], other[step] = swap(chunk[-step]), swap(chunk[step])

    for step in range(1, reach):
        join(step, low[-reach], high[reach])
    join(reach)
    last = lax.optimization_barrier((chunk["low"], chunk["high"], other[-reach], other[reach]))
    chunk["low"], chunk["high"], other[-reach], other[reach] = last
    other["low"], other["high"] = swap(chunk["low"]), swap(chunk["high"])
    names = ["low", "high", *[k for step in range(reach, 0, -1) for k in (-step, step)], 0]
    rows = [other[k] for k in names] + [chunk[k] for k in names[:-1]] + [low[0], high[0]]
    heights = [other[k].shape[0] for k in names]
    outs = partial_sums(tables, rows, heights * 2, roots, early)
    other, own = dict(zip(names, outs)), dict(zip(names, outs[len(names) :]))

    here = lambda k: own[k].astype(F32) + swap(other[k]).astype(F32)
    sent = here("low").astype(BF16), here("high").astype(BF16)
    pieces = slots * CUT
    shares = [0] + [pieces * part // 16 for part in (2, 7, 12, 16)]
    shares = [0] * (reach - 3) + shares if reach >= 3 else [0] * (reach + 1) + [pieces]
    done = None
    for step in range(reach, -1, -1):
        low, high = back(sent[0]), ahead(sent[1])
        base, stop = shares[reach - step : reach - step + 2]
        if stop > base:
            now = lax.optimization_barrier((*tables, *sent))[: len(tables)]
            done = update_stats(now, rows, stats, base, stop - base, done)
            low, high, done = lax.optimization_barrier((low, high, done))
        low, high = low.astype(F32), high.astype(F32)
        if step == reach:
            low = jnp.pad(low, ((0, width - half), (0, 0)))
            high = jnp.pad(high, ((half, 0), (0, 0)))
        if step:
            sent = (here(-step) + low).astype(BF16), (here(step) + high).astype(BF16)
    return done, (here(0) + low + high).astype(BF16)


def solution(mesh):
    placed = (
        P(("groups", "row"), None),
        P(("groups", "row"), None, None),
        P(("groups", "row"), None, None),
        P(),
    )
    return jax.shard_map(
        body,
        mesh=mesh,
        in_specs=placed,
        out_specs=(P(("groups", "row"), None, None), P(("groups", "row"), None)),
        check_vma=False,
    )
```
